32 devices in a mesh: scene: 2 (over y), bins: 4 (over z), az: 4 (over x, core).
Axes of the slice: x: 2, y: 2, z: 4, core: 2. Of those that a mesh axis runs over, the one named last changes fastest.
Arguments:
- raw_echoes: bfloat16 [2, 8, 512, 16384], P(None, ('scene', 'az'), 'bins'), parts along dimension 1, may hold values from -6 to 6
- range_phase: float32 [16384], replicated, may hold values from -3.140625 to 3.140625
- band_start: int32 [16384], replicated, may hold values from 0 to 16447, as said below
- band_weight: bfloat16 [8, 16384], replicated, may hold values from -0.25 to 0.75
- intersection_length: int32 [16384], P('bins'), may hold values from 32 to 128
- azimuth_rate: float32 [16384], P('bins'), may hold values from 0.25 to 2
Outputs:
- focused_image: bfloat16 [2, 8, 512, 16384], P(None, ('scene', 'az'), None, 'bins'), parts along dimension 1
The draws below stay inside these ranges and needn't reach their ends.
There are 2 independent parts, one for each index of `scene`. The reference program is written for one: setup_inputs(seed, part) draws one part's arguments, and reference() takes and returns one part's arrays. A program takes and returns all parts, laid end to end along the dimension named above; an argument that names none is the same for every part. Nothing has to cross between parts.
Inputs may be any that keep to these rules, and one draw needn't show every extreme that they name: band_start[b] - b lies between 0 and 64 for every range bin b.
All inputs are finite; a program needn't handle non-finite values.
Results may differ from the reference program's by a relative error of at most 0.02.
Values may be sent and summed in bfloat16 or wider, within the bound.
A program may use at most 128 MiB of HBM per device.

```python
import math
import jax
import jax.numpy as jnp
from jax import lax

NR = 16384
SUBP = 512
OVLMAX = 128
TAPS = 8
SHIFT = 64
N_AZ = 4


def draw_band_start(key, part):
    first_key = jax.random.fold_in(key, 11)
    offsets = jax.random.randint(first_key, (NR,), 0, SHIFT + 1)
    positions = jnp.arange(NR)
    offsets = jnp.where(positions == NR - 1, SHIFT, offsets)
    offsets = jnp.where(positions == 0, 0, offsets)
    return (positions + offsets).astype(jnp.int32)


def draw_intersection_length(key, part):
    first_key, second_key = jax.random.split(jax.random.fold_in(key, 23))
    lengths = jax.random.randint(first_key, (NR,), OVLMAX // 4, OVLMAX + 1)
    chosen = jax.random.randint(second_key, (), 0, NR)
    lengths = jnp.where(jnp.arange(NR) == chosen, OVLMAX, lengths)
    return lengths.astype(jnp.int32)


def block_scale(rng, shape, shards, low, high):
    level = 1.0
    for axis_at, parts in shards:
        heights = jax.random.uniform(jax.random.fold_in(jax.random.fold_in(rng, 6), axis_at), (parts,), jnp.float32, low / len(shards), high / len(shards))
        level = level * jnp.repeat(jnp.exp(heights), shape[axis_at] // parts).reshape((-1,) + (1,) * (len(shape) - 1 - axis_at))
    return level


def bell_draw(own_key, shape, spread, reach, cuts=(), held_as=jnp.bfloat16):
    gain = block_scale(own_key, shape, cuts, -0.22, 0.18) if cuts else 1.0
    values = jax.random.normal(own_key, shape, jnp.float32) * spread * gain
    return jnp.minimum(jnp.maximum(values, -reach), reach).astype(held_as)


def setup_inputs(seed: int = 0, part: int = 0) -> dict:
    splits = jax.random.split(jax.random.key(seed), 7)
    part_splits = jax.random.split(jax.random.fold_in(splits[6], part), 7)
    raw_echoes = bell_draw(part_splits[0], (2, N_AZ, SUBP, NR), 1.0, 6.0, ((1, 4), (2, 4)))
    range_phase = jnp.clip(jax.random.uniform(splits[1], (NR,), jnp.float32, -3.140625, 3.140625), -3.140625, 3.140625)
    band_start = draw_band_start(jax.random.fold_in(splits[6], 71), part)
    band_weight = jnp.clip(jax.random.uniform(splits[3], (TAPS, NR), jnp.float32, -0.25, 0.75), -0.25, 0.75).astype(jnp.bfloat16)
    intersection_length = draw_intersection_length(jax.random.fold_in(splits[6], 71), part)
    azimuth_rate = jnp.clip(jnp.exp(math.log(2.0) - 2.0794415 * jax.random.uniform(splits[5], (NR,), jnp.float32) ** block_scale(splits[5], (NR,), ((0, 4),), -0.2, 0.2)), 0.25, 2.0)
    return {"raw_echoes": raw_echoes, "range_phase": range_phase, "band_start": band_start, "band_weight": band_weight, "intersection_length": intersection_length, "azimuth_rate": azimuth_rate}


def round_pair(values):
    return jnp.real(values).astype(jnp.bfloat16), jnp.imag(values).astype(jnp.bfloat16)


def widen(real_part, imag_part):
    return real_part.astype(jnp.float32) + 1j * imag_part.astype(jnp.float32)


def reference(raw_echoes, range_phase, band_start, band_weight, intersection_length, azimuth_rate):
    range_filter = jnp.exp(-1j * range_phase)

    def migrate_lines(component):
        padded = jnp.pad(component.astype(jnp.float32), ((0, 0), (0, 128)))
        summed = jnp.zeros(component.shape, jnp.float32)
        for tap_index in range(TAPS):
            picked = jnp.take(padded, band_start + tap_index, axis=1)
            summed = summed + band_weight[tap_index].astype(jnp.float32)[None, :] * picked
        return summed.astype(jnp.bfloat16)

    def range_section(echo_block):
        spectrum = jnp.fft.fft(widen(echo_block[0], echo_block[1]), axis=1) * range_filter[None, :]
        filt_real, filt_imag = round_pair(spectrum)
        lines = jnp.fft.ifft(widen(filt_real, filt_imag), axis=1)
        comp_real, comp_imag = round_pair(lines)
        return jnp.stack([migrate_lines(comp_real), migrate_lines(comp_imag)])

    migrated = lax.map(range_section, jnp.moveaxis(raw_echoes, 1, 0))
    head_lines = jnp.concatenate([migrated[1:, :, :OVLMAX], jnp.zeros_like(migrated[:1, :, :OVLMAX])], axis=0)
    pulses = jnp.arange(SUBP + OVLMAX)[:, None]
    inside = (pulses < SUBP) | (pulses - SUBP < intersection_length[None, :])
    doppler = jnp.arange(SUBP + OVLMAX)
    signed = jnp.where(2 * doppler >= SUBP + OVLMAX, doppler - (SUBP + OVLMAX), doppler).astype(jnp.float32)
    phase_angle = math.pi * azimuth_rate[None, :] * (signed * signed)[:, None] / (SUBP + OVLMAX)
    azimuth_filter = jnp.exp(-1j * phase_angle)

    def azimuth_section(operands):
        own_lines, next_lines = operands
        aperture = jnp.concatenate([own_lines, next_lines], axis=1)
        aperture = jnp.where(inside[None], aperture, jnp.zeros((), jnp.bfloat16))
        spectrum = jnp.fft.fft(widen(aperture[0], aperture[1]), axis=0) * azimuth_filter
        spec_real, spec_imag = round_pair(spectrum)
        image_pair = jnp.fft.ifft(widen(spec_real, spec_imag), axis=0)[:SUBP]
        image_real, image_imag = round_pair(image_pair)
        return jnp.stack([image_real, image_imag])

    images = lax.map(azimuth_section, (migrated, head_lines))
    return jnp.moveaxis(images, 0, 1)
```

```python
import functools
import math

import jax
import jax.numpy as jnp
import numpy as np
from jax import lax
from jax.experimental import pallas as pl
from jax.experimental.pallas import tpu as pltpu
from jax.sharding import PartitionSpec as P

OVLMAX = 128
LANES = 128
CHUNK = 16
GROUP = 512
TILE = 256
EARLY_DIVISOR = 4
MESH = pl.DeviceIdType.MESH

COS_POLY = (
    1.0,
    -19.739208221435547,
    64.93939208984375,
    -85.45665740966797,
    60.242130279541016,
    -26.4046688079834,
    7.800131320953369,
    -1.453112244606018,
)
SIN_POLY = (
    6.2831854820251465,
    -41.34170150756836,
    81.6052474975586,
    -76.70580291748047,
    42.05775451660156,
    -15.086565017700195,
    3.7813189029693604,
    -0.6207787394523621,
)


def cosine_table(rows, cols, length):
    angle = 2.0 * math.pi / length * ((np.arange(rows)[:, None] * np.arange(cols)[None, :]) % length)
    return np.cos(angle), np.sin(angle)


def unit_turn(turns):
    r = turns - jnp.round(turns)
    s = r * r
    cosine = jnp.full_like(s, COS_POLY[-1])
    for value in COS_POLY[-2::-1]:
        cosine = cosine * s + value
    sine = jnp.full_like(s, SIN_POLY[-1])
    for value in SIN_POLY[-2::-1]:
        sine = sine * s + value
    return cosine, sine * r


def mm(left, right):
    return jnp.dot(left, right, preferred_element_type=jnp.float32)


def send_order(count):
    return sorted(range(1, count), key=lambda step: abs(2 * step - count))


def focus_kernel(
    n_bins,
    n_az,
    raw,
    filt,
    starts,
    weights,
    lengths,
    rates,
    dft,
    twiddle,
    az_table,
    out,
    raw_buf,
    xs,
    os_,
    send,
    recv,
    heads,
    ap,
    sp,
    out_buf,
    raw_sem,
    out_sem,
    early_send,
    early_recv,
    early_local,
    late_send,
    late_recv,
    late_local,
    head_send,
    head_recv,
):
    line = raw.shape[2]
    own = raw.shape[1]
    cols = out.shape[2]
    lines = out.shape[1]
    length = lines + OVLMAX
    chunks = own // CHUNK
    groups = cols // GROUP
    early = max(1, groups // EARLY_DIVISOR)
    early_width = early * GROUP + LANES
    me = lax.axis_index("bins")
    az = lax.axis_index("az")
    has_prev = az > 0
    has_next = az < n_az - 1
    order = send_order(n_bins)
    radix = line // LANES

    barrier = pltpu.get_barrier_semaphore()
    for step in range(1, n_bins):
        peer = lax.rem(me + step, n_bins)
        pl.semaphore_signal(barrier, inc=1, device_id={"bins": peer}, device_id_type=MESH)

    @pl.when(has_prev)
    def _():
        pl.semaphore_signal(barrier, inc=1, device_id={"az": az - 1}, device_id_type=MESH)

    @pl.when(has_next)
    def _():
        pl.semaphore_signal(barrier, inc=1, device_id={"az": az + 1}, device_id_type=MESH)

    def raw_copy(chunk, slot):
        return pltpu.make_async_copy(
            raw.at[:, pl.ds(pl.multiple_of(chunk * CHUNK, CHUNK), CHUNK), :], raw_buf.at[slot], raw_sem.at[slot]
        )

    raw_copy(0, 0).start()
    send[:, :, pl.ds(line, LANES)] = jnp.zeros((2, own, LANES), jnp.bfloat16)

    @pl.when(jnp.logical_not(has_next))
    def _():
        heads[...] = jnp.zeros(heads.shape, jnp.bfloat16)

    def early_copy(chunk, step, index):
        rows = pl.multiple_of(chunk * CHUNK, CHUNK)
        peer = lax.rem(me + step, n_bins)
        return pltpu.make_async_remote_copy(
            src_ref=send.at[:, pl.ds(rows, CHUNK), pl.ds(pl.multiple_of(peer * cols, LANES), early_width)],
            dst_ref=recv.at[:, pl.ds(pl.multiple_of(me * own + rows, CHUNK), CHUNK), pl.ds(0, early_width)],
            send_sem=early_send.at[chunk, index],
            recv_sem=early_recv.at[chunk, index],
            device_id={"bins": peer},
            device_id_type=MESH,
        )

    def early_own(chunk):
        rows = pl.multiple_of(chunk * CHUNK, CHUNK)
        return pltpu.make_async_copy(
            send.at[:, pl.ds(rows, CHUNK), pl.ds(pl.multiple_of(me * cols, LANES), early_width)],
            recv.at[:, pl.ds(pl.multiple_of(me * own + rows, CHUNK), CHUNK), pl.ds(0, early_width)],
            early_local.at[chunk],
        )

    def late_copy(group, step, index):
        peer = lax.rem(me + step, n_bins)
        first = group * GROUP + LANES
        return pltpu.make_async_remote_copy(
            src_ref=send.at[:, :, pl.ds(pl.multiple_of(peer * cols + first, LANES), GROUP)],
            dst_ref=recv.at[:, pl.ds(pl.multiple_of(me * own, CHUNK), own), pl.ds(pl.multiple_of(first, LANES), GROUP)],
            send_sem=late_send.at[group, index],
            recv_sem=late_recv.at[group, index],
            device_id={"bins": peer},
            device_id_type=MESH,
        )

    def late_own(group):
        first = group * GROUP + LANES
        return pltpu.make_async_copy(
            send.at[:, :, pl.ds(pl.multiple_of(me * cols + first, LANES), GROUP)],
            recv.at[:, pl.ds(pl.multiple_of(me * own, CHUNK), own), pl.ds(pl.multiple_of(first, LANES), GROUP)],
            late_local.at[group],
        )

    def head_copy(group, first, width):
        span = pl.ds(first, width)
        return pltpu.make_async_remote_copy(
            src_ref=recv.at[:, pl.ds(0, OVLMAX), span],
            dst_ref=heads.at[:, :, span],
            send_sem=head_send.at[group],
            recv_sem=head_recv.at[group],
            device_id={"az": az - 1},
            device_id_type=MESH,
        )

    def late_first(group):
        return pl.multiple_of(group * GROUP + LANES, LANES)

    def compress(chunk, carry):
        slot = lax.rem(chunk, 2)
        raw_copy(chunk, slot).wait()

        @pl.when(chunk + 1 < chunks)
        def _():
            raw_copy(chunk + 1, 1 - slot).start()

        def spread(index, inner):
            span = pl.ds(pl.multiple_of(index * LANES, LANES), LANES)
            for part in range(2):
                xs[part, pl.ds(index, CHUNK, radix), :] = raw_buf[slot, part, :, span].astype(jnp.float32)
            return inner

        lax.fori_loop(0, radix, spread, 0, unroll=8)

        def pulses(pair, inner):
            columns = []
            for which in range(2):
                rows = pl.ds(pl.multiple_of((2 * pair + which) * radix, radix), radix)
                columns.append(
                    jnp.concatenate([xs[0, rows, :], xs[1, rows, :]], axis=0).astype(jnp.bfloat16)
                )
            first = mm(dft[0], jnp.concatenate(columns, axis=1))
            tc, ts = twiddle[0], twiddle[1]
            stacked = []
            for which in range(2):
                re = first[:radix, which * LANES : (which + 1) * LANES]
                im = first[radix:, which * LANES : (which + 1) * LANES]
                stacked.append(
                    jnp.concatenate([re * tc + im * ts, im * tc - re * ts], axis=1).astype(jnp.bfloat16)
                )
            spectrum = mm(jnp.concatenate(stacked, axis=0), dft[1])
            fc, fs = filt[0], filt[1]
            stacked = []
            for which in range(2):
                re = spectrum[which * radix : (which + 1) * radix, :LANES]
                im = spectrum[which * radix : (which + 1) * radix, LANES:]
                stacked.append(
                    jnp.concatenate([re * fc + im * fs, im * fc - re * fs], axis=1).astype(jnp.bfloat16)
                )
            back = mm(jnp.concatenate(stacked, axis=0), dft[2])
            columns = []
            for which in range(2):
                re = back[which * radix : (which + 1) * radix, :LANES]
                im = back[which * radix : (which + 1) * radix, LANES:]
                columns.append(
                    jnp.concatenate([re * tc - im * ts, im * tc + re * ts], axis=0).astype(jnp.bfloat16)
                )
            last = mm(dft[3], jnp.concatenate(columns, axis=1))
            for which in range(2):
                for part in range(2):
                    os_[part, pl.ds(2 * pair + which, radix, CHUNK), :] = last[
                        part * radix : (part + 1) * radix, which * LANES : (which + 1) * LANES
                    ]
            return inner

        lax.fori_loop(0, CHUNK // 2, pulses, 0)
        rows_out = pl.ds(pl.multiple_of(chunk * CHUNK, CHUNK), CHUNK)

        def gather(index, inner):
            span = pl.ds(pl.multiple_of(index * LANES, LANES), LANES)
            rows = pl.ds(pl.multiple_of(index * CHUNK, CHUNK), CHUNK)
            for part in range(2):
                send[part, rows_out, span] = os_[part, rows, :].astype(jnp.bfloat16)
            return inner

        lax.fori_loop(0, radix, gather, 0, unroll=8)

        @pl.when(chunk == 0)
        def _():
            pl.semaphore_wait(barrier, n_bins - 1 + has_prev.astype(jnp.int32) + has_next.astype(jnp.int32))

        for index, step in enumerate(order):
            early_copy(chunk, step, index).start()
        early_own(chunk).start()
        return carry

    lax.fori_loop(0, chunks, compress, 0)

    def send_late(group, carry):
        for index, step in enumerate(order):
            late_copy(group, step, index).start()
        late_own(group).start()
        return carry

    lax.fori_loop(early, groups, send_late, 0)

    def out_copy(group, slot):
        return pltpu.make_async_copy(
            out_buf.at[slot],
            out.at[:, :, pl.ds(pl.multiple_of(group * GROUP, GROUP), GROUP)],
            out_sem.at[slot],
        )

    def focus(group, carry):
        @pl.when(group == 0)
        def _():
            def arrived(chunk, inner):
                for index, step in enumerate(order):
                    early_copy(chunk, step, index).wait_recv()
                early_own(chunk).wait()
                return inner

            lax.fori_loop(0, chunks, arrived, 0)

            @pl.when(has_prev)
            def _():
                head_copy(0, 0, early_width).start()

            @pl.when(has_next)
            def _():
                head_copy(0, 0, early_width).wait_recv()

        @pl.when(group >= early)
        def _():
            late_own(group).wait()
            for index, step in enumerate(order):
                late_copy(group, step, index).wait_recv()

            @pl.when(has_prev)
            def _():
                head_copy(group, late_first(group), GROUP).start()

            @pl.when(has_next)
            def _():
                head_copy(group, late_first(group), GROUP).wait_recv()

        slot = lax.rem(group, 2)

        @pl.when(group >= 2)
        def _():
            out_copy(group - 2, slot).wait()

        def tile(index, inner):
            for block in range(TILE // LANES):
                base = pl.multiple_of(group * GROUP + index * TILE + block * LANES, LANES)
                whole = pl.ds(pl.multiple_of(me * cols + base, LANES), LANES)
                offset = starts[:, whole] - (me * cols + base)
                taps = weights[:, whole].astype(jnp.float32)
                place = lax.broadcasted_iota(jnp.int32, (2 * LANES, LANES), 0) - offset
                band = jnp.zeros((2 * LANES, LANES), jnp.float32)
                for tap in range(taps.shape[0]):
                    band = jnp.where(place == tap, taps[tap : tap + 1, :], band)
                band = band.astype(jnp.bfloat16)
                inside = lax.broadcasted_iota(jnp.int32, (OVLMAX, LANES), 0) < lengths[:, pl.ds(base, LANES)]
                window = pl.ds(base, 2 * LANES)
                here = pl.ds(block * LANES, LANES)
                for part in range(2):
                    ap[part, pl.ds(0, lines), here] = mm(recv[part, :, window], band).astype(jnp.bfloat16)
                    tail = jnp.where(inside, mm(heads[part, :, window], band), 0.0)
                    ap[part, pl.ds(lines, OVLMAX), here] = tail.astype(jnp.bfloat16)
            re, im = ap[0], ap[1]
            spec_re = mm(az_table[:, : 2 * length], jnp.concatenate([re, -im], axis=0))
            spec_im = mm(az_table[:, length:], jnp.concatenate([re, im], axis=0))
            span = pl.ds(pl.multiple_of(group * GROUP + index * TILE, TILE), TILE)
            doppler = lax.broadcasted_iota(jnp.int32, (length, TILE), 0)
            signed = jnp.where(2 * doppler >= length, doppler - length, doppler)
            square = (signed * signed).astype(jnp.float32)
            fc, fs = unit_turn(square * (rates[:, span] * (0.5 / length)))
            sp[0] = (spec_re * fc + spec_im * fs).astype(jnp.bfloat16)
            sp[1] = (spec_im * fc - spec_re * fs).astype(jnp.bfloat16)
            re, im = sp[0], sp[1]
            here = pl.ds(pl.multiple_of(index * TILE, TILE), TILE)
            image = mm(az_table[:lines, : 2 * length], jnp.concatenate([re, im], axis=0))
            out_buf[slot, 0, :, here] = (image * (1.0 / length)).astype(jnp.bfloat16)
            image = mm(az_table[:lines, length:], jnp.concatenate([-re, im], axis=0))
            out_buf[slot, 1, :, here] = (image * (1.0 / length)).astype(jnp.bfloat16)
            return inner

        lax.fori_loop(0, GROUP // TILE, tile, 0)
        out_copy(group, slot).start()
        return carry

    lax.fori_loop(0, groups, focus, 0)
    for group in range(max(0, groups - 2), groups):
        out_copy(group, group % 2).wait()

    def early_done(chunk, carry):
        for index, step in enumerate(order):
            early_copy(chunk, step, index).wait_send()
        return carry

    lax.fori_loop(0, chunks, early_done, 0)

    def late_done(group, carry):
        for index, step in enumerate(order):
            late_copy(group, step, index).wait_send()

        @pl.when(has_prev)
        def _():
            head_copy(group, late_first(group), GROUP).wait_send()

        return carry

    lax.fori_loop(early, groups, late_done, 0)

    @pl.when(has_prev)
    def _():
        head_copy(0, 0, early_width).wait_send()


def shards(n_bins, n_az, raw_echoes, range_phase, band_start, band_weight, intersection_length, azimuth_rate):
    raw = raw_echoes[:, 0]
    own, line = raw.shape[1], raw.shape[2]
    cols = intersection_length.shape[0]
    lines = own * n_bins
    length = lines + OVLMAX
    radix = line // LANES
    groups = cols // GROUP
    chunks = own // CHUNK
    early_width = max(1, groups // EARLY_DIVISOR) * GROUP + LANES

    fr, fi = cosine_table(radix, radix, radix)
    fi = -fi
    dft = np.stack(
        [
            np.block([[fr, -fi], [fi, fr]]),
            np.block([[fr, fi], [-fi, fr]]),
            np.block([[fr, -fi], [fi, fr]]),
            np.block([[fr, fi], [-fi, fr]]) / line,
        ]
    )
    twiddle = np.stack(cosine_table(radix, LANES, line)).astype(np.float32)
    ar, ai = cosine_table(length, length, length)
    az_table = np.concatenate([ar, -ai, ar], axis=1)
    angle = range_phase.reshape(LANES, radix).T
    filt = jnp.stack([jnp.cos(angle), jnp.sin(angle)])

    vmem = pl.BlockSpec(memory_space=pltpu.VMEM)
    hbm = pl.BlockSpec(memory_space=pl.ANY)
    dma = pltpu.SemaphoreType.DMA
    bf16, f32 = jnp.bfloat16, jnp.float32
    image = pl.pallas_call(
        functools.partial(focus_kernel, n_bins, n_az),
        out_shape=jax.ShapeDtypeStruct((2, lines, cols), bf16),
        in_specs=[hbm] + [vmem] * 8,
        out_specs=hbm,
        scratch_shapes=[
            pltpu.VMEM((2, 2, CHUNK, line), bf16),
            pltpu.VMEM((2, CHUNK * radix, LANES), f32),
            pltpu.VMEM((2, CHUNK * radix, LANES), f32),
            pltpu.VMEM((2, own, line + LANES), bf16),
            pltpu.VMEM((2, lines, cols + LANES), bf16),
            pltpu.VMEM((2, OVLMAX, cols + LANES), bf16),
            pltpu.VMEM((2, length, TILE), bf16),
            pltpu.VMEM((2, length, TILE), bf16),
            pltpu.VMEM((2, 2, lines, GROUP), bf16),
            dma((2,)),
            dma((2,)),
            dma((chunks, n_bins - 1)),
            dma((chunks, n_bins - 1)),
            dma((chunks,)),
            dma((groups, n_bins - 1)),
            dma((groups, n_bins - 1)),
            dma((groups,)),
            dma((groups,)),
            dma((groups,)),
        ],
        compiler_params=pltpu.CompilerParams(
            collective_id=0, has_side_effects=True, vmem_limit_bytes=60 * 1024 * 1024
        ),
    )(
        raw,
        filt,
        band_start.reshape(1, line),
        band_weight,
        intersection_length.reshape(1, cols),
        azimuth_rate.reshape(1, cols),
        jnp.asarray(dft, bf16),
        jnp.asarray(twiddle),
        jnp.asarray(az_table, bf16),
    )
    return image[:, None]


def solution(mesh):
    in_specs = (P(None, ("scene", "az"), "bins", None), P(), P(), P(), P("bins"), P("bins"))
    out_specs = P(None, ("scene", "az"), None, "bins")
    body = functools.partial(shards, mesh.shape["bins"], mesh.shape["az"])
    return jax.shard_map(body, mesh=mesh, in_specs=in_specs, out_specs=out_specs, check_vma=False)
```

```python
import functools
import math

import jax
import jax.numpy as jnp
import numpy as np
from jax import lax
from jax.experimental import pallas as pl
from jax.experimental.pallas import tpu as pltpu
from jax.sharding import PartitionSpec as P

OVLMAX = 128
LANES = 128
CHUNK = 16
GROUP = 256
TILE = 256
EARLY_SHARE = 5 / 16
MESH = pl.DeviceIdType.MESH

COS_POLY = (
    1.0,
    -19.739208221435547,
    64.93939208984375,
    -85.45665740966797,
    60.242130279541016,
    -26.4046688079834,
    7.800131320953369,
    -1.453112244606018,
)
SIN_POLY = (
    6.2831854820251465,
    -41.34170150756836,
    81.6052474975586,
    -76.70580291748047,
    42.05775451660156,
    -15.086565017700195,
    3.7813189029693604,
    -0.6207787394523621,
)


def cosine_table(rows, cols, length):
    angle = 2.0 * math.pi / length * ((np.arange(rows)[:, None] * np.arange(cols)[None, :]) % length)
    return np.cos(angle), np.sin(angle)


def unit_turn(turns):
    r = turns - jnp.round(turns)
    s = r * r
    cosine = jnp.full_like(s, COS_POLY[-1])
    for value in COS_POLY[-2::-1]:
        cosine = cosine * s + value
    sine = jnp.full_like(s, SIN_POLY[-1])
    for value in SIN_POLY[-2::-1]:
        sine = sine * s + value
    return cosine, sine * r


def mm(left, right):
    return jnp.dot(left, right, preferred_element_type=jnp.float32)


def send_order(count):
    return sorted(range(1, count), key=lambda step: abs(2 * step - count))


def focus_kernel(
    n_bins,
    n_az,
    raw,
    filt,
    starts,
    weights,
    lengths,
    rates,
    dft,
    twiddle,
    az_table,
    out,
    raw_buf,
    xs,
    os_,
    send,
    recv,
    heads,
    ap,
    sp,
    out_buf,
    raw_sem,
    out_sem,
    early_send,
    early_recv,
    early_local,
    late_send,
    late_recv,
    late_local,
    head_send,
    head_recv,
):
    line = raw.shape[2]
    own = raw.shape[1]
    cols = out.shape[2]
    lines = out.shape[1]
    length = lines + OVLMAX
    chunks = own // CHUNK
    groups = cols // GROUP
    early = max(1, int(groups * EARLY_SHARE))
    early_width = early * GROUP + LANES
    me = lax.axis_index("bins")
    az = lax.axis_index("az")
    has_prev = az > 0
    has_next = az < n_az - 1
    order = send_order(n_bins)
    radix = line // LANES

    barrier = pltpu.get_barrier_semaphore()
    for step in range(1, n_bins):
        peer = lax.rem(me + step, n_bins)
        pl.semaphore_signal(barrier, inc=1, device_id={"bins": peer}, device_id_type=MESH)

    @pl.when(has_prev)
    def _():
        pl.semaphore_signal(barrier, inc=1, device_id={"az": az - 1}, device_id_type=MESH)

    @pl.when(has_next)
    def _():
        pl.semaphore_signal(barrier, inc=1, device_id={"az": az + 1}, device_id_type=MESH)

    def raw_copy(chunk, slot):
        return pltpu.make_async_copy(
            raw.at[:, pl.ds(pl.multiple_of(chunk * CHUNK, CHUNK), CHUNK), :], raw_buf.at[slot], raw_sem.at[slot]
        )

    raw_copy(0, 0).start()
    send[:, :, pl.ds(line, LANES)] = jnp.zeros((2, own, LANES), jnp.bfloat16)

    @pl.when(jnp.logical_not(has_next))
    def _():
        heads[...] = jnp.zeros(heads.shape, jnp.bfloat16)

    def early_copy(chunk, step, index):
        rows = pl.multiple_of(chunk * CHUNK, CHUNK)
        peer = lax.rem(me + step, n_bins)
        return pltpu.make_async_remote_copy(
            src_ref=send.at[:, pl.ds(rows, CHUNK), pl.ds(pl.multiple_of(peer * cols, LANES), early_width)],
            dst_ref=recv.at[:, pl.ds(pl.multiple_of(me * own + rows, CHUNK), CHUNK), pl.ds(0, early_width)],
            send_sem=early_send.at[chunk, index],
            recv_sem=early_recv.at[chunk, index],
            device_id={"bins": peer},
            device_id_type=MESH,
        )

    def early_own(chunk):
        rows = pl.multiple_of(chunk * CHUNK, CHUNK)
        return pltpu.make_async_copy(
            send.at[:, pl.ds(rows, CHUNK), pl.ds(pl.multiple_of(me * cols, LANES), early_width)],
            recv.at[:, pl.ds(pl.multiple_of(me * own + rows, CHUNK), CHUNK), pl.ds(0, early_width)],
            early_local.at[chunk],
        )

    def late_copy(group, step, index):
        peer = lax.rem(me + step, n_bins)
        first = group * GROUP + LANES
        return pltpu.make_async_remote_copy(
            src_ref=send.at[:, :, pl.ds(pl.multiple_of(peer * cols + first, LANES), GROUP)],
            dst_ref=recv.at[:, pl.ds(pl.multiple_of(me * own, CHUNK), own), pl.ds(pl.multiple_of(first, LANES), GROUP)],
            send_sem=late_send.at[group, index],
            recv_sem=late_recv.at[group, index],
            device_id={"bins": peer},
            device_id_type=MESH,
        )

    def late_own(group):
        first = group * GROUP + LANES
        return pltpu.make_async_copy(
            send.at[:, :, pl.ds(pl.multiple_of(me * cols + first, LANES), GROUP)],
            recv.at[:, pl.ds(pl.multiple_of(me * own, CHUNK), own), pl.ds(pl.multiple_of(first, LANES), GROUP)],
            late_local.at[group],
        )

    def head_copy(group, first, width):
        span = pl.ds(first, width)
        return pltpu.make_async_remote_copy(
            src_ref=recv.at[:, pl.ds(0, OVLMAX), span],
            dst_ref=heads.at[:, :, span],
            send_sem=head_send.at[group],
            recv_sem=head_recv.at[group],
            device_id={"az": az - 1},
            device_id_type=MESH,
        )

    def late_first(group):
        return pl.multiple_of(group * GROUP + LANES, LANES)

    def compress(chunk, carry):
        slot = lax.rem(chunk, 2)
        raw_copy(chunk, slot).wait()

        @pl.when(chunk + 1 < chunks)
        def _():
            raw_copy(chunk + 1, 1 - slot).start()

        def spread(index, inner):
            span = pl.ds(pl.multiple_of(index * LANES, LANES), LANES)
            for part in range(2):
                xs[part, pl.ds(index, CHUNK, radix), :] = raw_buf[slot, part, :, span].astype(jnp.float32)
            return inner

        lax.fori_loop(0, radix, spread, 0, unroll=8)

        def pulses(pair, inner):
            columns = []
            for which in range(2):
                rows = pl.ds(pl.multiple_of((2 * pair + which) * radix, radix), radix)
                columns.append(
                    jnp.concatenate([xs[0, rows, :], xs[1, rows, :]], axis=0).astype(jnp.bfloat16)
                )
            first = mm(dft[0], jnp.concatenate(columns, axis=1))
            tc, ts = twiddle[0], twiddle[1]
            stacked = []
            for which in range(2):
                re = first[:radix, which * LANES : (which + 1) * LANES]
                im = first[radix:, which * LANES : (which + 1) * LANES]
                stacked.append(
                    jnp.concatenate([re * tc + im * ts, im * tc - re * ts], axis=1).astype(jnp.bfloat16)
                )
            spectrum = mm(jnp.concatenate(stacked, axis=0), dft[1])
            fc, fs = filt[0], filt[1]
            stacked = []
            for which in range(2):
                re = spectrum[which * radix : (which + 1) * radix, :LANES]
                im = spectrum[which * radix : (which + 1) * radix, LANES:]
                stacked.append(
                    jnp.concatenate([re * fc + im * fs, im * fc - re * fs], axis=1).astype(jnp.bfloat16)
                )
            back = mm(jnp.concatenate(stacked, axis=0), dft[2])
            columns = []
            for which in range(2):
                re = back[which * radix : (which + 1) * radix, :LANES]
                im = back[which * radix : (which + 1) * radix, LANES:]
                columns.append(
                    jnp.concatenate([re * tc - im * ts, im * tc + re * ts], axis=0).astype(jnp.bfloat16)
                )
            last = mm(dft[3], jnp.concatenate(columns, axis=1))
            for which in range(2):
                for part in range(2):
                    os_[part, pl.ds(2 * pair + which, radix, CHUNK), :] = last[
                        part * radix : (part + 1) * radix, which * LANES : (which + 1) * LANES
                    ]
            return inner

        lax.fori_loop(0, CHUNK // 2, pulses, 0, unroll=4)
        rows_out = pl.ds(pl.multiple_of(chunk * CHUNK, CHUNK), CHUNK)

        def gather(index, inner):
            span = pl.ds(pl.multiple_of(index * LANES, LANES), LANES)
            rows = pl.ds(pl.multiple_of(index * CHUNK, CHUNK), CHUNK)
            for part in range(2):
                send[part, rows_out, span] = os_[part, rows, :].astype(jnp.bfloat16)
            return inner

        lax.fori_loop(0, radix, gather, 0, unroll=8)

        @pl.when(chunk == 0)
        def _():
            pl.semaphore_wait(barrier, n_bins - 1 + has_prev.astype(jnp.int32) + has_next.astype(jnp.int32))

        for index, step in enumerate(order):
            early_copy(chunk, step, index).start()
        early_own(chunk).start()
        return carry

    lax.fori_loop(0, chunks, compress, 0)

    def send_late(group, carry):
        for index, step in enumerate(order):
            late_copy(group, step, index).start()
        late_own(group).start()
        return carry

    lax.fori_loop(early, groups, send_late, 0)

    def out_copy(group, slot):
        return pltpu.make_async_copy(
            out_buf.at[slot],
            out.at[:, :, pl.ds(pl.multiple_of(group * GROUP, GROUP), GROUP)],
            out_sem.at[slot],
        )

    def focus(group, carry):
        @pl.when(group == 0)
        def _():
            def arrived(chunk, inner):
                for index, step in enumerate(order):
                    early_copy(chunk, step, index).wait_recv()
                early_own(chunk).wait()
                return inner

            lax.fori_loop(0, chunks, arrived, 0)

            @pl.when(has_prev)
            def _():
                head_copy(0, 0, early_width).start()

            @pl.when(has_next)
            def _():
                head_copy(0, 0, early_width).wait_recv()

        @pl.when(group >= early)
        def _():
            late_own(group).wait()
            for index, step in enumerate(order):
                late_copy(group, step, index).wait_recv()

            @pl.when(has_prev)
            def _():
                head_copy(group, late_first(group), GROUP).start()

            @pl.when(has_next)
            def _():
                head_copy(group, late_first(group), GROUP).wait_recv()

        slot = lax.rem(group, 2)

        @pl.when(group >= 2)
        def _():
            out_copy(group - 2, slot).wait()

        def tile(index, inner):
            for block in range(TILE // LANES):
                base = pl.multiple_of(group * GROUP + index * TILE + block * LANES, LANES)
                whole = pl.ds(pl.multiple_of(me * cols + base, LANES), LANES)
                offset = starts[:, whole] - (me * cols + base)
                taps = weights[:, whole].astype(jnp.float32)
                place = lax.broadcasted_iota(jnp.int32, (2 * LANES, LANES), 0) - offset
                band = jnp.zeros((2 * LANES, LANES), jnp.float32)
                for tap in range(taps.shape[0]):
                    band = jnp.where(place == tap, taps[tap : tap + 1, :], band)
                band = band.astype(jnp.bfloat16)
                inside = lax.broadcasted_iota(jnp.int32, (OVLMAX, LANES), 0) < lengths[:, pl.ds(base, LANES)]
                window = pl.ds(base, 2 * LANES)
                here = pl.ds(block * LANES, LANES)
                for part in range(2):
                    ap[part, pl.ds(0, lines), here] = mm(recv[part, :, window], band).astype(jnp.bfloat16)
                    tail = jnp.where(inside, mm(heads[part, :, window], band), 0.0)
                    ap[part, pl.ds(lines, OVLMAX), here] = tail.astype(jnp.bfloat16)
            re, im = ap[0], ap[1]
            spec_re = mm(az_table[:, : 2 * length], jnp.concatenate([re, -im], axis=0))
            spec_im = mm(az_table[:, length:], jnp.concatenate([re, im], axis=0))
            span = pl.ds(pl.multiple_of(group * GROUP + index * TILE, TILE), TILE)
            doppler = lax.broadcasted_iota(jnp.int32, (length, TILE), 0)
            signed = jnp.where(2 * doppler >= length, doppler - length, doppler)
            square = (signed * signed).astype(jnp.float32)
            fc, fs = unit_turn(square * (rates[:, span] * (0.5 / length)))
            sp[0] = (spec_re * fc + spec_im * fs).astype(jnp.bfloat16)
            sp[1] = (spec_im * fc - spec_re * fs).astype(jnp.bfloat16)
            re, im = sp[0], sp[1]
            here = pl.ds(pl.multiple_of(index * TILE, TILE), TILE)
            image = mm(az_table[:lines, : 2 * length], jnp.concatenate([re, im], axis=0))
            out_buf[slot, 0, :, here] = (image * (1.0 / length)).astype(jnp.bfloat16)
            image = mm(az_table[:lines, length:], jnp.concatenate([-re, im], axis=0))
            out_buf[slot, 1, :, here] = (image * (1.0 / length)).astype(jnp.bfloat16)
            return inner

        lax.fori_loop(0, GROUP // TILE, tile, 0)
        out_copy(group, slot).start()
        return carry

    lax.fori_loop(0, groups, focus, 0)
    for group in range(max(0, groups - 2), groups):
        out_copy(group, group % 2).wait()

    def early_done(chunk, carry):
        for index, step in enumerate(order):
            early_copy(chunk, step, index).wait_send()
        return carry

    lax.fori_loop(0, chunks, early_done, 0)

    def late_done(group, carry):
        for index, step in enumerate(order):
            late_copy(group, step, index).wait_send()

        @pl.when(has_prev)
        def _():
            head_copy(group, late_first(group), GROUP).wait_send()

        return carry

    lax.fori_loop(early, groups, late_done, 0)

    @pl.when(has_prev)
    def _():
        head_copy(0, 0, early_width).wait_send()


def shards(n_bins, n_az, raw_echoes, range_phase, band_start, band_weight, intersection_length, azimuth_rate):
    raw = raw_echoes[:, 0]
    own, line = raw.shape[1], raw.shape[2]
    cols = intersection_length.shape[0]
    lines = own * n_bins
    length = lines + OVLMAX
    radix = line // LANES
    groups = cols // GROUP
    chunks = own // CHUNK

    fr, fi = cosine_table(radix, radix, radix)
    fi = -fi
    dft = np.stack(
        [
            np.block([[fr, -fi], [fi, fr]]),
            np.block([[fr, fi], [-fi, fr]]),
            np.block([[fr, -fi], [fi, fr]]),
            np.block([[fr, fi], [-fi, fr]]) / line,
        ]
    )
    twiddle = np.stack(cosine_table(radix, LANES, line)).astype(np.float32)
    ar, ai = cosine_table(length, length, length)
    az_table = np.concatenate([ar, -ai, ar], axis=1)
    angle = range_phase.reshape(LANES, radix).T
    filt = jnp.stack([jnp.cos(angle), jnp.sin(angle)])

    vmem = pl.BlockSpec(memory_space=pltpu.VMEM)
    hbm = pl.BlockSpec(memory_space=pl.ANY)
    dma = pltpu.SemaphoreType.DMA
    bf16, f32 = jnp.bfloat16, jnp.float32
    image = pl.pallas_call(
        functools.partial(focus_kernel, n_bins, n_az),
        out_shape=jax.ShapeDtypeStruct((2, lines, cols), bf16),
        in_specs=[hbm] + [vmem] * 8,
        out_specs=hbm,
        scratch_shapes=[
            pltpu.VMEM((2, 2, CHUNK, line), bf16),
            pltpu.VMEM((2, CHUNK * radix, LANES), f32),
            pltpu.VMEM((2, CHUNK * radix, LANES), f32),
            pltpu.VMEM((2, own, line + LANES), bf16),
            pltpu.VMEM((2, lines, cols + LANES), bf16),
            pltpu.VMEM((2, OVLMAX, cols + LANES), bf16),
            pltpu.VMEM((2, length, TILE), bf16),
            pltpu.VMEM((2, length, TILE), bf16),
            pltpu.VMEM((2, 2, lines, GROUP), bf16),
            dma((2,)),
            dma((2,)),
            dma((chunks, n_bins - 1)),
            dma((chunks, n_bins - 1)),
            dma((chunks,)),
            dma((groups, n_bins - 1)),
            dma((groups, n_bins - 1)),
            dma((groups,)),
            dma((groups,)),
            dma((groups,)),
        ],
        compiler_params=pltpu.CompilerParams(
            collective_id=0, has_side_effects=True, vmem_limit_bytes=60 * 1024 * 1024
        ),
    )(
        raw,
        filt,
        band_start.reshape(1, line),
        band_weight,
        intersection_length.reshape(1, cols),
        azimuth_rate.reshape(1, cols),
        jnp.asarray(dft, bf16),
        jnp.asarray(twiddle),
        jnp.asarray(az_table, bf16),
    )
    return image[:, None]


def solution(mesh):
    in_specs = (P(None, ("scene", "az"), "bins", None), P(), P(), P(), P("bins"), P("bins"))
    out_specs = P(None, ("scene", "az"), None, "bins")
    body = functools.partial(shards, mesh.shape["bins"], mesh.shape["az"])
    return jax.shard_map(body, mesh=mesh, in_specs=in_specs, out_specs=out_specs, check_vma=False)
```
